32 devices in a mesh: grp: 4 (over z), sep: 8 (over y, x, core).
Axes of the slice: x: 2, y: 2, z: 4, core: 2. Of those that a mesh axis runs over, the one named last changes fastest.
Arguments:
- tiles: bfloat16 [4, 256, 64, 128], P('grp', 'sep'), may hold values from 0.0099487305 to 0.29882812
- tile_front: int32 [4, 256, 1], P('grp', 'sep'), may hold values from 0 to 7; in each aligned block of 32 rows (0 to 31, 32 to 63, ..., all dimensions but the last counted through in order) at most 8 rows name the same one
- tile_pos: int32 [4, 256], P('grp', 'sep'), may hold values from 0 to 29
- front_slot: int32 [4, 8], P('grp'), may hold values from 0 to 7, as said below
- front_parent: int32 [4, 8], P('grp'), may hold values from 0 to 7, as said below
- pivot: float32 [4, 8, 640], P('grp'), may hold values from 4 to 40
Outputs:
- factor: float32 [4, 8, 640, 512], P('grp', 'sep')
- sep_schur: float32 [8, 128, 128], P('sep')
The draws below stay inside these ranges and needn't reach their ends.
Inputs may be any that keep to these rules, and one draw needn't show every extreme that they name: `tile_front`: at most 8 of the tiles held by one device belong to one front. `front_slot`: each group's row is a permutation of 0 to 7. (front_parent[g, f] - front_slot[g, f]) modulo 8 is one of 0, 1, 7 and 4; in every group each of these four occurs.
All inputs are finite; a program needn't handle non-finite values.
Results may differ from the reference program's by a relative error of at most 0.0003.
Values may be sent and summed in bfloat16 or wider, within the bound.
A program may use at most 64 MiB of HBM per device.

```python
import math
import jax
import jax.numpy as jnp
import numpy as np
from jax import lax

TR = 64
TC = 128
TILE_DEV = 32
POS = 30
FRONTS = 8
TILES = 256
CAP = 8
ORDER = 640
N_GRP = 4


def front_maps(key):
    keys = jax.random.split(jax.random.fold_in(key, 101), N_GRP)
    slots = jax.vmap(lambda single: jax.random.permutation(single, FRONTS))(keys).astype(jnp.int32)
    choices_drawn = jax.random.randint(jax.random.fold_in(key, 202), (N_GRP, FRONTS), 0, 4)
    forced = jnp.arange(FRONTS, dtype=jnp.int32)[None, :]
    choices_drawn = jnp.where(forced < 4, forced, choices_drawn)
    table = jnp.array([0, 1, FRONTS - 1, FRONTS // 2], jnp.int32)
    offsets = jnp.sum(jnp.where(choices_drawn[:, :, None] == jnp.arange(4, dtype=jnp.int32)[None, None, :], table[None, None, :], 0), 2)
    parents = (slots + offsets) % FRONTS
    return (slots, parents.astype(jnp.int32))


def draw_front_slot(key, part):
    return front_maps(key)[0]


def draw_front_parent(key, part):
    return front_maps(key)[1]


def place_ends(drawn, own_key, low, largest):
    spot = [jax.random.randint(jax.random.fold_in(own_key, axis), (), 0, length) for axis, length in enumerate(drawn.shape)]
    longest = drawn.shape.index(max(drawn.shape))
    neighbour = spot[:longest] + [(spot[longest] + 1) % drawn.shape[longest]] + spot[longest + 1:]
    return drawn.at[tuple(spot)].set(low).at[tuple(neighbour)].set(largest)


def shard_levels(key, shape, shards, low, top_value):
    def one(dim, parts):
        steps = jax.random.uniform(jax.random.fold_in(jax.random.fold_in(key, 6), dim), (parts,), jnp.float32, low / len(shards), top_value / len(shards))
        return jnp.repeat(jnp.exp(steps), shape[dim] // parts).reshape((-1,) + (1,) * (len(shape) - dim - 1))

    gain = one(*shards[0])
    for cut in shards[1:]:
        gain = gain * one(*cut)
    return gain


def shared_out(own_key, own, number, rows, number_of, top, reach, slope):
    order = jax.random.permutation(own_key, number_of)
    crowded, usual = load_shares(number_of, rows * top, reach, slope, True), load_shares(number_of, rows * top, reach, slope, False)
    places = jnp.arange(number_of)

    def named(sizes, offset_by):
        used = int((sizes > 0).sum())
        fixed = max(1, used // 4)
        passed = fixed + (places - fixed + offset_by * (used - fixed)) % max(1, number_of - fixed)
        return jnp.zeros((number_of,), jnp.int32).at[order[jnp.where(places < fixed, places, passed)]].set(jnp.asarray(sizes, jnp.int32))

    sizes = jnp.where(number % 4 == 0, named(crowded, number // 4), named(usual, number - number // 4 - 1))
    mixed = jax.random.permutation(jax.random.fold_in(own, 3), number_of)
    giver, sink = mixed[0:number_of // 2 * 2:2], mixed[1:number_of // 2 * 2:2]
    slack = jnp.minimum(sizes[giver] - 1, reach - sizes[sink]) // 2
    slack = jnp.where((giver == order[0]) | (sink == order[0]) | (sizes[sink] == 0), 0, jnp.maximum(slack, 0))
    passed = jax.random.randint(jax.random.fold_in(own, 4), (number_of // 2,), 0, 1 << 20) % (slack + 1)
    sizes = sizes.at[giver].add(-passed).at[sink].add(passed)
    members = jnp.searchsorted(jnp.cumsum(sizes), jnp.arange(rows * top), side="right").astype(jnp.int32)
    listing = members.reshape(top, rows).T
    listing = listing[jax.random.permutation(jax.random.fold_in(own, 1), rows)]
    offset_by = jax.random.randint(jax.random.fold_in(own, 2), (rows, 1), 0, top)
    return jnp.take_along_axis(listing, (jnp.arange(top)[None, :] + offset_by) % top, axis=1)


def load_shares(number_of, total, bound, lean, full):
    weights = [(1 << 20) // math.isqrt(grade ** lean) + 1 for grade in range(1, number_of + 1)]
    largest = bound if full else min(bound, max(-(-total // number_of), total * weights[0] // sum(weights)))
    least = 1 if total - largest >= number_of - 1 else 0
    counts, spare = [largest] + [least] * (number_of - 1), total - largest - least * (number_of - 1)
    while spare > 0:
        movable = [i for i in range(1, number_of) if counts[i] < largest] or [i for i in range(1, number_of) if counts[i] < bound]
        whole, remaining = sum([weights[i] for i in movable]), spare
        for i in movable:
            more = min(bound - counts[i], max(1, remaining * weights[i] // whole), spare)
            counts[i] = counts[i] + more
            spare = spare - more
    return np.array(counts)


def setup_inputs(seed: int = 0) -> dict:
    splits = jax.random.split(jax.random.key(seed), 7)
    tiles = jnp.clip(jnp.exp(math.log(0.29882812) - 3.4024236 * jax.random.uniform(splits[0], (N_GRP, TILES, TR, TC), jnp.float32) ** shard_levels(splits[0], (N_GRP, TILES, TR, TC), ((0, 4), (1, 8)), -0.2, 0.2)), 0.0099487305, 0.29882812).astype(jnp.bfloat16)
    tile_front_keys = jax.random.split(jax.random.fold_in(splits[1], 1), N_GRP * TILES // TILE_DEV)
    tile_front_turns = jax.random.permutation(jax.random.fold_in(splits[1], 3), N_GRP * TILES // TILE_DEV)
    tile_front = jax.vmap(lambda own, number: shared_out(jax.random.fold_in(splits[1], 2), own, number, TILE_DEV, FRONTS, 1, CAP, 2))(tile_front_keys, tile_front_turns).reshape((N_GRP, TILES, 1))
    tile_pos = place_ends(jax.random.randint(splits[2], (N_GRP, TILES), 0, POS), jax.random.fold_in(splits[2], 1), 0, POS - 1).astype(jnp.int32)
    front_slot = draw_front_slot(jax.random.fold_in(splits[6], 71), 0)
    front_parent = draw_front_parent(jax.random.fold_in(splits[6], 71), 0)
    pivot = jnp.clip(jnp.exp(math.log(40.0) - 2.3025851 * jax.random.uniform(splits[5], (N_GRP, FRONTS, ORDER), jnp.float32) ** shard_levels(splits[5], (N_GRP, FRONTS, ORDER), ((0, 4),), -0.2, 0.2)), 4.0, 40.0)
    return dict(tiles=tiles, tile_front=tile_front, tile_pos=tile_pos, front_slot=front_slot, front_parent=front_parent, pivot=pivot)


def tile_arrangement(rows, column_indices):
    row_count = 5 * column_indices // rows
    position = np.zeros((row_count, 5), np.int32)
    present = np.zeros((row_count, 5), np.float32)
    number = 0
    for row_block in range(row_count):
        for col_block in range(row_block * rows // column_indices + 1):
            position[row_block, col_block] = number
            present[row_block, col_block] = 1.0
            number += 1
    return (position, present)

def front_factor(summed, pivots, rows, column_indices):
    position, present = tile_arrangement(rows, column_indices)
    order = 5 * column_indices
    elimination_count = 4 * column_indices
    blocks = summed[position] * jnp.asarray(present, jnp.float32)[:, :, None, None]
    full = blocks.transpose(0, 2, 1, 3).reshape(order, order)
    mixed = 0.5 * (full + full.T) * (1.0 - jnp.eye(order, dtype=jnp.float32))
    front_matrix = jnp.diag(pivots + jnp.sum(mixed, 1)) - mixed
    lower_triangle = jnp.linalg.cholesky(front_matrix[:elimination_count, :elimination_count])
    under_diagonal = jax.scipy.linalg.solve_triangular(lower_triangle, front_matrix[elimination_count:, :elimination_count].T, lower=True).T
    schur = jnp.dot(under_diagonal, under_diagonal.T, precision=lax.Precision.HIGHEST)
    return (jnp.concatenate([lower_triangle, under_diagonal], 0), schur)

def reference(tiles, tile_front, tile_pos, front_slot, front_parent, pivot):
    rows = tiles.shape[2]
    column_indices = tiles.shape[3]
    fronts = front_slot.shape[1]

    def per_group(items):
        group_tiles, group_front, group_pos, slots, parents, pivots = items
        labels = (group_front[:, 0] * POS + group_pos).astype(jnp.int32)
        summed = jax.ops.segment_sum(group_tiles.astype(jnp.float32), labels, num_segments=fronts * POS)
        summed = summed.reshape(fronts, POS, rows, column_indices)

        def per_front(pair):
            return front_factor(pair[0], pair[1], rows, column_indices)
        leaf_factors, schurs = lax.map(per_front, (summed, pivots))
        placed = jnp.zeros_like(leaf_factors).at[slots].set(leaf_factors)
        sums = jax.ops.segment_sum(schurs, parents, num_segments=fronts)
        return (placed, sums)
    placed, sums = lax.map(per_group, (tiles, tile_front, tile_pos, front_slot, front_parent, pivot))
    return (placed, jnp.sum(sums, 0))
```

```python
import functools
import jax
import jax.numpy as jnp
from jax import lax
from jax.experimental import pallas as pl
from jax.experimental.pallas import tpu as pltpu
from jax.sharding import PartitionSpec as P

MESH = pl.DeviceIdType.MESH

PANEL = 8


def dot_nt(a, b):
    return lax.dot_general(a, b, (((1,), (1,)), ((), ())), precision=lax.Precision.HIGHEST, preferred_element_type=jnp.float32)


def lanes(x, j):
    return jnp.broadcast_to(x[:, j : j + 1], x.shape)


def sublanes(x, r):
    return jnp.broadcast_to(x[r : r + 1, :], x.shape)


def factor_diagonal(a_ref, u_ref, w_ref):
    size = a_ref.shape[0]
    panels = size // PANEL
    sub = lax.broadcasted_iota(jnp.int32, (PANEL, size), 0)
    lane = lax.broadcasted_iota(jnp.int32, (PANEL, size), 1)
    a = [a_ref[PANEL * i : PANEL * (i + 1), :] for i in range(panels)]
    w = [jnp.where(lane == sub + PANEL * i, 1.0, 0.0) for i in range(panels)]
    for p in range(panels):
        j0 = PANEL * p
        cols = [lanes(a[p], j0 + r) for r in range(PANEL)]
        b = [[sublanes(cols[r], s) for s in range(r + 1)] for r in range(PANEL)]
        ta = [sublanes(a[p], r) for r in range(PANEL)]
        tw = [sublanes(w[p], r) for r in range(PANEL)]
        inv = [None] * PANEL
        n = [[None] * PANEL for _ in range(PANEL)]
        for r in range(PANEL):
            inv[r] = 1.0 / b[r][r]
            for s in range(r + 1, PANEL):
                n[s][r] = b[s][r] * inv[r]
            for s in range(r + 1, PANEL):
                for t in range(r + 1, s + 1):
                    b[s][t] = b[s][t] - n[s][r] * b[t][r]
            for s in range(r + 1, PANEL):
                ta[s] = ta[s] - n[s][r] * ta[r]
                tw[s] = tw[s] - n[s][r] * tw[r]
        u = ta[0] * lax.rsqrt(b[0][0])
        v = tw[0] * lax.rsqrt(b[0][0])
        for r in range(1, PANEL):
            root = lax.rsqrt(b[r][r])
            u = jnp.where(sub == r, ta[r] * root, u)
            v = jnp.where(sub == r, tw[r] * root, v)
        u_ref[j0 : j0 + PANEL, :] = jnp.where(lane >= sub + j0, u, 0.0)
        w_ref[j0 : j0 + PANEL, :] = v
        if p + 1 < panels:
            ya = [None] * PANEL
            yw = [None] * PANEL
            for r in reversed(range(PANEL)):
                ya[r] = ta[r] * inv[r]
                yw[r] = tw[r] * inv[r]
            for r in reversed(range(PANEL)):
                for s in range(r):
                    ya[s] = ya[s] - n[r][s] * ya[r]
                    yw[s] = yw[s] - n[r][s] * yw[r]
            for i in range(p + 1, panels):
                for s in range(PANEL):
                    c = lanes(a[i], j0 + s)
                    a_new = c * ya[s] if s == 0 else a_new + c * ya[s]
                    w_new = c * yw[s] if s == 0 else w_new + c * yw[s]
                a[i] = a[i] - a_new
                w[i] = w[i] - w_new


def front_kernel(rows, offsets, codes, distance, tiles, pivots, factor_ref, pieces_ref, acc, diag, up, winv, schur_ref):
    size = tiles.shape[2]
    blocks = pivots.shape[0]
    elim = blocks - 1
    acc[...] = jnp.zeros_like(acc)

    def add_tile(t, carry):
        code = codes[t]
        c = code & 7
        r = pl.multiple_of((code >> 3) * rows, rows)
        acc[c, pl.ds(r, rows), :] += tiles[t].astype(jnp.float32)
        return carry

    lax.fori_loop(0, tiles.shape[0], add_tile, 0, unroll=4)

    sub = lax.broadcasted_iota(jnp.int32, (size, size), 0)
    lane = lax.broadcasted_iota(jnp.int32, (size, size), 1)

    def span(i):
        return slice(i * size, (i + 1) * size)

    row_sums = [jnp.zeros((size, 1), jnp.float32) for _ in range(blocks)]
    for j in range(elim):
        f = acc[j, span(j), :]
        mixed = jnp.where(sub == lane, 0.0, 0.5 * (f + f.T))
        sums = pivots[j : j + 1, :] + jnp.sum(mixed, 0, keepdims=True)
        for i in range(j + 1, blocks):
            half = 0.5 * acc[j, span(i), :]
            sums = sums + jnp.sum(half, 0, keepdims=True)
            if i < elim:
                row_sums[i] = row_sums[i] + jnp.sum(half, 1, keepdims=True)
            acc[j, span(i), :] = -half
        acc[j, span(j), :] = jnp.where(sub == lane, sums + row_sums[j], -mixed)

    def step(k, carry):
        diag[...] = acc[k, pl.ds(pl.multiple_of(k * size, size), size), :]
        factor_diagonal(diag, up, winv)
        for kk in range(elim):
            @pl.when(k == kk)
            def _():
                w = winv[...]
                factor_ref[span(kk), span(kk)] = up[...].T
                for j in range(kk + 1, elim):
                    factor_ref[span(kk), span(j)] = jnp.zeros((size, size), jnp.float32)
                below = dot_nt(acc[kk, (kk + 1) * size : blocks * size, :], w)
                factor_ref[(kk + 1) * size : blocks * size, span(kk)] = below
                for j in range(kk + 1, elim):
                    o = (j - kk - 1) * size
                    acc[j, j * size : blocks * size, :] -= dot_nt(below[o:, :], below[o : o + size, :])
                last = below[(elim - kk - 1) * size :, :]
                if kk == 0:
                    schur_ref[...] = dot_nt(last, last)
                else:
                    schur_ref[...] += dot_nt(last, last)
        return carry

    lax.fori_loop(0, elim, step, 0)
    for n, offset in enumerate(offsets):
        pieces_ref[n] = jnp.where(distance[0] == offset, schur_ref[...], 0.0)


def front_call(codes, distance, tiles, pivots, rows, columns, offsets):
    blocks = pivots.shape[0]
    return pl.pallas_call(
        functools.partial(front_kernel, rows, offsets),
        out_shape=(
            jax.ShapeDtypeStruct((blocks * columns, (blocks - 1) * columns), jnp.float32),
            jax.ShapeDtypeStruct((len(offsets), columns, columns), jnp.float32),
        ),
        in_specs=[
            pl.BlockSpec(memory_space=pltpu.SMEM),
            pl.BlockSpec(memory_space=pltpu.SMEM),
            pl.BlockSpec(memory_space=pltpu.VMEM),
            pl.BlockSpec(memory_space=pltpu.VMEM),
        ],
        out_specs=(pl.BlockSpec(memory_space=pltpu.VMEM), pl.BlockSpec(memory_space=pltpu.VMEM)),
        scratch_shapes=[
            pltpu.VMEM((blocks, blocks * columns + rows, columns), jnp.float32),
            pltpu.VMEM((columns, columns), jnp.float32),
            pltpu.VMEM((columns, columns), jnp.float32),
            pltpu.VMEM((columns, columns), jnp.float32),
            pltpu.VMEM((columns, columns), jnp.float32),
        ],
    )(codes, distance, tiles, pivots)


def schur_kernel(groups, width, offsets, pieces, total, arrived, gathered, send1, recv1, send2, recv2):
    grp = lax.axis_index("grp")
    sep = lax.axis_index("sep")
    barrier = pltpu.get_barrier_semaphore()
    for offset in offsets[1:]:
        pl.semaphore_signal(barrier, inc=1, device_id=(grp, (sep + offset) % width), device_id_type=MESH)
    for hop in range(1, groups):
        pl.semaphore_signal(barrier, inc=1, device_id=((grp + hop) % groups, sep), device_id_type=MESH)
    pl.semaphore_wait(barrier, len(offsets) - 1 + groups - 1)
    first = []
    for n, offset in enumerate(offsets[1:]):
        copy = pltpu.make_async_remote_copy(
            src_ref=pieces.at[n + 1],
            dst_ref=arrived.at[n],
            send_sem=send1.at[n],
            recv_sem=recv1.at[n],
            device_id=(grp, (sep + offset) % width),
            device_id_type=MESH,
        )
        copy.start()
        first.append(copy)
    for copy in first:
        copy.wait_recv()
    local = pieces[0]
    for n in range(len(first)):
        local = local + arrived[n]
    gathered[grp] = local
    second = []
    for hop in range(1, groups):
        copy = pltpu.make_async_remote_copy(
            src_ref=gathered.at[grp],
            dst_ref=gathered.at[grp],
            send_sem=send2.at[hop - 1],
            recv_sem=recv2.at[hop - 1],
            device_id=((grp + hop) % groups, sep),
            device_id_type=MESH,
        )
        copy.start()
        second.append(copy)
    for copy in first:
        copy.wait_send()
    for copy in second:
        copy.wait_recv()
    summed = gathered[0]
    for g in range(1, groups):
        summed = summed + gathered[g]
    total[...] = summed
    for copy in second:
        copy.wait_send()


def schur_call(pieces, groups, width, offsets):
    _, size, _ = pieces.shape
    partners = len(offsets) - 1
    return pl.pallas_call(
        functools.partial(schur_kernel, groups, width, offsets),
        out_shape=jax.ShapeDtypeStruct((size, size), jnp.float32),
        in_specs=[pl.BlockSpec(memory_space=pltpu.VMEM)],
        out_specs=pl.BlockSpec(memory_space=pltpu.VMEM),
        scratch_shapes=[
            pltpu.VMEM((partners, size, size), jnp.float32),
            pltpu.VMEM((groups, size, size), jnp.float32),
            pltpu.SemaphoreType.DMA((partners,)),
            pltpu.SemaphoreType.DMA((partners,)),
            pltpu.SemaphoreType.DMA((groups - 1,)),
            pltpu.SemaphoreType.DMA((groups - 1,)),
        ],
        compiler_params=pltpu.CompilerParams(collective_id=1, has_side_effects=True),
    )(pieces)


def position_codes(positions, rows, columns):
    ratio = columns // rows
    row_count = 5 * ratio
    starts = [0]
    for r in range(row_count):
        starts.append(starts[-1] + r // ratio + 1)
    row = sum((positions >= starts[r]).astype(jnp.int32) for r in range(1, row_count))
    begin = sum(jnp.where(positions >= starts[r], starts[r] - starts[r - 1], 0) for r in range(1, row_count))
    return row * 8 + positions - begin, row_count * 8


def body(groups, width, tiles, tile_front, tile_pos, front_slot, front_parent, pivot):
    myself = lax.axis_index("sep")
    held = tiles.shape[1]
    rows = tiles.shape[2]
    columns = tiles.shape[3]
    fronts = front_slot.shape[1]
    room = max(2, -(-2 * held // width))
    offsets = (0, 1, width - 1, width // 2)
    slots = front_slot[0]
    parents = front_parent[0]
    front_ids = jnp.arange(fronts, dtype=jnp.int32)
    owner_of = jnp.sum(jnp.where(tile_front[0] == front_ids[None, :], slots[None, :], 0), 1)
    target = (owner_of[:, None] == jnp.arange(width, dtype=jnp.int32)[None, :]).astype(jnp.int32)
    rank = jnp.sum(target * (jnp.cumsum(target, 0) - 1), 1)
    place = owner_of * room + rank
    codes, empty = position_codes(tile_pos[0], rows, columns)
    outgoing = jnp.zeros((width * room, rows, columns), jnp.bfloat16).at[place].set(tiles[0])
    labels = jnp.full((width * room,), empty, jnp.int32).at[place].set(codes)
    arrived, labels = (
        lax.all_to_all(outgoing.reshape(width, room, rows, columns), "sep", split_axis=0, concat_axis=0, tiled=True),
        lax.all_to_all(labels.reshape(width, room), "sep", split_axis=0, concat_axis=0, tiled=True),
    )
    arrived = arrived.reshape(width * room, rows, columns)
    labels = labels.reshape(width * room)
    mine = slots == myself
    pivots = jnp.sum(jnp.where(mine[:, None], pivot[0], 0.0), 0).reshape(-1, columns)
    parent = jnp.sum(jnp.where(mine, parents, 0))
    distance = jnp.reshape((parent - myself) % width, (1,))
    factor, pieces = front_call(labels, distance, arrived, pivots, rows, columns, offsets)
    total = schur_call(pieces, groups, width, offsets)
    return (factor[None, None], total[None])


def solution(mesh):
    placed = (
        P("grp", "sep", None, None),
        P("grp", "sep", None),
        P("grp", "sep"),
        P("grp", None),
        P("grp", None),
        P("grp", None, None),
    )
    return jax.shard_map(
        functools.partial(body, mesh.shape["grp"], mesh.shape["sep"]),
        mesh=mesh,
        in_specs=placed,
        out_specs=(P("grp", "sep", None, None), P("sep", None, None)),
        check_vma=False,
    )
```

```python
import functools
import jax
import jax.numpy as jnp
from jax import lax
from jax.experimental import pallas as pl
from jax.experimental.pallas import tpu as pltpu
from jax.sharding import PartitionSpec as P

MESH = pl.DeviceIdType.MESH

PANEL = 8
GRANT = 20 * 1024 * 1024


def dot_nt(a, b):
    return lax.dot_general(a, b, (((1,), (1,)), ((), ())), precision=lax.Precision.HIGHEST, preferred_element_type=jnp.float32)


def lanes(x, j):
    return jnp.broadcast_to(x[:, j : j + 1], x.shape)


def sublanes(x, r):
    return jnp.broadcast_to(x[r : r + 1, :], x.shape)


def factor_diagonal(a_ref, u_ref, w_ref):
    size = a_ref.shape[0]
    panels = size // PANEL
    sub = lax.broadcasted_iota(jnp.int32, (PANEL, size), 0)
    lane = lax.broadcasted_iota(jnp.int32, (PANEL, size), 1)
    a = [a_ref[PANEL * i : PANEL * (i + 1), :] for i in range(panels)]
    w = [jnp.where(lane == sub + PANEL * i, 1.0, 0.0) for i in range(panels)]
    for p in range(panels):
        j0 = PANEL * p
        cols = [lanes(a[p], j0 + r) for r in range(PANEL)]
        b = [[sublanes(cols[r], s) for s in range(r + 1)] for r in range(PANEL)]
        ta = [sublanes(a[p], r) for r in range(PANEL)]
        tw = [sublanes(w[p], r) for r in range(PANEL)]
        inv = [None] * PANEL
        n = [[None] * PANEL for _ in range(PANEL)]
        for r in range(PANEL):
            inv[r] = 1.0 / b[r][r]
            for s in range(r + 1, PANEL):
                n[s][r] = b[s][r] * inv[r]
            for s in range(r + 1, PANEL):
                for t in range(r + 1, s + 1):
                    b[s][t] = b[s][t] - n[s][r] * b[t][r]
            for s in range(r + 1, PANEL):
                ta[s] = ta[s] - n[s][r] * ta[r]
                tw[s] = tw[s] - n[s][r] * tw[r]
        u = ta[0] * lax.rsqrt(b[0][0])
        v = tw[0] * lax.rsqrt(b[0][0])
        for r in range(1, PANEL):
            root = lax.rsqrt(b[r][r])
            u = jnp.where(sub == r, ta[r] * root, u)
            v = jnp.where(sub == r, tw[r] * root, v)
        u_ref[j0 : j0 + PANEL, :] = jnp.where(lane >= sub + j0, u, 0.0)
        w_ref[j0 : j0 + PANEL, :] = v
        if p + 1 < panels:
            ya = [None] * PANEL
            yw = [None] * PANEL
            for r in reversed(range(PANEL)):
                ya[r] = ta[r] * inv[r]
                yw[r] = tw[r] * inv[r]
            for r in reversed(range(PANEL)):
                for s in range(r):
                    ya[s] = ya[s] - n[r][s] * ya[r]
                    yw[s] = yw[s] - n[r][s] * yw[r]
            for i in range(p + 1, panels):
                for s in range(PANEL):
                    c = lanes(a[i], j0 + s)
                    a_new = c * ya[s] if s == 0 else a_new + c * ya[s]
                    w_new = c * yw[s] if s == 0 else w_new + c * yw[s]
                a[i] = a[i] - a_new
                w[i] = w[i] - w_new


def front_kernel(offsets, room, slots, parents, labels, tiles, pivots, factor_ref, pieces_ref, codes, acc, diag, up, winv, schur_ref, sem):
    width, _, rows, size = tiles.shape
    blocks = acc.shape[0]
    elim = blocks - 1
    me = lax.axis_index("sep")
    fetch = pltpu.make_async_copy(labels, codes, sem)
    fetch.start()
    acc[...] = jnp.zeros_like(acc)
    front = 0
    parent = 0
    for f in range(pivots.shape[0]):
        hit = slots[f] == me
        front = jnp.where(hit, f, front)
        parent = jnp.where(hit, parents[f], parent)
    distance = parent - me
    distance = jnp.where(distance < 0, distance + width, distance)
    fetch.wait()

    def add_tiles(s, carry):
        for t in range(room):
            code = codes[s, 0, t]
            r = pl.multiple_of((code >> 3) * rows, rows)
            acc[code & 7, pl.ds(r, rows), :] += tiles[s, t].astype(jnp.float32)
        return carry

    lax.fori_loop(0, width, add_tiles, 0)

    sub = lax.broadcasted_iota(jnp.int32, (size, size), 0)
    lane = lax.broadcasted_iota(jnp.int32, (size, size), 1)

    def span(i):
        return slice(i * size, (i + 1) * size)

    picked = lax.broadcasted_iota(jnp.int32, (pivots.shape[0], size), 0) == front
    row_sums = [jnp.zeros((size, 1), jnp.float32) for _ in range(blocks)]
    for j in range(elim):
        f = acc[j, span(j), :]
        mixed = jnp.where(sub == lane, 0.0, 0.5 * (f + f.T))
        sums = jnp.sum(jnp.where(picked, pivots[:, span(j)], 0.0), 0, keepdims=True) + jnp.sum(mixed, 0, keepdims=True)
        for i in range(j + 1, blocks):
            half = 0.5 * acc[j, span(i), :]
            sums = sums + jnp.sum(half, 0, keepdims=True)
            if i < elim:
                row_sums[i] = row_sums[i] + jnp.sum(half, 1, keepdims=True)
            acc[j, span(i), :] = -half
        acc[j, span(j), :] = jnp.where(sub == lane, sums + row_sums[j], -mixed)

    def step(k, carry):
        diag[...] = acc[k, pl.ds(pl.multiple_of(k * size, size), size), :]
        factor_diagonal(diag, up, winv)
        for kk in range(elim):
            @pl.when(k == kk)
            def _():
                w = winv[...]
                factor_ref[span(kk), span(kk)] = up[...].T
                for j in range(kk + 1, elim):
                    factor_ref[span(kk), span(j)] = jnp.zeros((size, size), jnp.float32)
                below = dot_nt(acc[kk, (kk + 1) * size : blocks * size, :], w)
                factor_ref[(kk + 1) * size : blocks * size, span(kk)] = below
                for j in range(kk + 1, elim):
                    o = (j - kk - 1) * size
                    acc[j, j * size : blocks * size, :] -= dot_nt(below[o:, :], below[o : o + size, :])
                last = below[(elim - kk - 1) * size :, :]
                if kk == 0:
                    schur_ref[...] = dot_nt(last, last)
                else:
                    schur_ref[...] += dot_nt(last, last)
        return carry

    lax.fori_loop(0, elim, step, 0)
    half = size // 2
    sub = lax.broadcasted_iota(jnp.int32, (half, size), 0)
    lane = lax.broadcasted_iota(jnp.int32, (half, size), 1)
    top = pltpu.roll(schur_ref[:half, :], half, 1)
    bottom = schur_ref[half:, :]
    packed = jnp.where((lane < half) | (lane - half > sub), bottom, top)
    tail = jnp.sum(jnp.where(lane - half == sub, bottom, 0.0), 0, keepdims=True)
    tail = jnp.broadcast_to(tail, (8, size))
    for n, offset in enumerate(offsets):
        pieces_ref[n, :half, :] = jnp.where(distance == offset, packed, 0.0)
        pieces_ref[n, half:, :] = jnp.where(distance == offset, tail, 0.0)


def vmem(count):
    return [pl.BlockSpec(memory_space=pltpu.VMEM)] * count


def smem(count):
    return [pl.BlockSpec(memory_space=pltpu.SMEM)] * count


def front_call(slots, parents, labels, tiles, pivots, offsets, room):
    width, _, rows, columns = tiles.shape
    order = pivots.shape[1]
    square = pltpu.VMEM((columns, columns), jnp.float32)
    return pl.pallas_call(
        functools.partial(front_kernel, offsets, room),
        out_shape=(
            jax.ShapeDtypeStruct((order, order - columns), jnp.float32),
            jax.ShapeDtypeStruct((len(offsets), columns // 2 + 8, columns), jnp.float32),
        ),
        in_specs=smem(2) + vmem(3),
        out_specs=vmem(2),
        scratch_shapes=[
            pltpu.SMEM(labels.shape, jnp.int32),
            pltpu.VMEM((order // columns, order + rows, columns), jnp.float32),
            square,
            square,
            square,
            square,
            pltpu.SemaphoreType.DMA,
        ],
        compiler_params=pltpu.CompilerParams(vmem_limit_bytes=GRANT),
        name="front",
    )(slots, parents, labels, tiles, pivots)


def position_codes(positions, rows, columns):
    ratio = columns // rows
    row_count = 5 * ratio
    starts = [0]
    for r in range(row_count):
        starts.append(starts[-1] + r // ratio + 1)
    row = sum((positions >= starts[r]).astype(jnp.int32) for r in range(1, row_count))
    begin = sum(jnp.where(positions >= starts[r], starts[r] - starts[r - 1], 0) for r in range(1, row_count))
    return jnp.where(positions < 0, row_count * 8, row * 8 + positions - begin)


def pack_kernel(fronts, positions, slots, tiles, outgoing, labels, counts):
    width = outgoing.shape[0]
    held, rows, columns = tiles.shape
    labels[...] = jnp.full(labels.shape, -1, jnp.int32)
    lane = lax.broadcasted_iota(jnp.int32, labels.shape[1:], 1)
    for d in range(width):
        counts[d] = 0

    def place(i, carry):
        owner = slots[fronts[i]]
        rank = counts[owner]
        counts[owner] = rank + 1
        outgoing[owner, rank] = tiles[i]
        labels[owner] = jnp.where(lane == rank, positions[i], labels[owner])
        return carry

    lax.fori_loop(0, held, place, 0, unroll=4)
    labels[...] = position_codes(labels[...], rows, columns)


def pack_call(fronts, positions, slots, tiles, width, room):
    held, rows, columns = tiles.shape
    return pl.pallas_call(
        pack_kernel,
        out_shape=(
            jax.ShapeDtypeStruct((width, room, rows, columns), tiles.dtype),
            jax.ShapeDtypeStruct((width, 1, 128), jnp.int32),
        ),
        in_specs=smem(3) + vmem(1),
        out_specs=vmem(2),
        scratch_shapes=[pltpu.SMEM((width,), jnp.int32)],
        compiler_params=pltpu.CompilerParams(vmem_limit_bytes=GRANT),
        name="pack",
    )(fronts, positions, slots, tiles)


def exchange_kernel(width, order, outgoing, labels, arrived, codes, send, recv, lsend, lrecv, own):
    grp = lax.axis_index("grp")
    sep = lax.axis_index("sep")
    barrier = pltpu.get_barrier_semaphore()
    bits = [1 << b for b in range(width.bit_length() - 1)]
    if width == 1 << len(bits):
        partners = [sum(((sep // b) % 2 + (h // b) % 2) % 2 * b for b in bits) for h in order]
    else:
        partners = [(sep + h) % width for h in order]
    for partner in partners:
        pl.semaphore_signal(barrier, inc=1, device_id=(grp, partner), device_id_type=MESH)
    mine = pltpu.make_async_copy(outgoing.at[sep], arrived.at[sep], own.at[0])
    mine.start()
    named = pltpu.make_async_copy(labels.at[sep], codes.at[sep], own.at[1])
    named.start()
    pl.semaphore_wait(barrier, width - 1)
    copies = []
    for n, partner in enumerate(partners):
        for src, dst, s, r in ((outgoing, arrived, send, recv), (labels, codes, lsend, lrecv)):
            copy = pltpu.make_async_remote_copy(
                src_ref=src.at[partner],
                dst_ref=dst.at[sep],
                send_sem=s.at[n],
                recv_sem=r.at[n],
                device_id=(grp, partner),
                device_id_type=MESH,
            )
            copy.start()
            copies.append(copy)
    mine.wait()
    named.wait()
    for copy in copies:
        copy.wait()


def exchange_call(outgoing, labels):
    width = outgoing.shape[0]
    partners = width - 1
    order = sorted(range(1, width), key=lambda h: (-bin(h >> 1).count("1"), h))
    return pl.pallas_call(
        functools.partial(exchange_kernel, width, order),
        out_shape=(
            jax.ShapeDtypeStruct(outgoing.shape, outgoing.dtype),
            jax.ShapeDtypeStruct(labels.shape, labels.dtype),
        ),
        in_specs=vmem(2),
        out_specs=vmem(2),
        scratch_shapes=[pltpu.SemaphoreType.DMA((partners,))] * 4 + [pltpu.SemaphoreType.DMA((2,))],
        compiler_params=pltpu.CompilerParams(collective_id=2, has_side_effects=True, vmem_limit_bytes=GRANT),
        name="exchange",
    )(outgoing, labels)


def unpack_kernel(packed, out):
    size = packed.shape[1]
    half = size // 2
    sub = lax.broadcasted_iota(jnp.int32, (half, size), 0)
    lane = lax.broadcasted_iota(jnp.int32, (half, size), 1)
    body = packed[:half, :]
    top = pltpu.roll(jnp.where((lane >= half) & (lane - half <= sub), body, 0.0), half, 1)
    bottom = jnp.where((lane < half) | (lane - half > sub), body, 0.0)
    lower = jnp.concatenate([top, bottom], 0)
    sub = lax.broadcasted_iota(jnp.int32, (size, size), 0)
    lane = lax.broadcasted_iota(jnp.int32, (size, size), 1)
    tail = jnp.where(lane >= half, packed[half : half + 1, :], 0.0)
    out[...] = lower + jnp.where(sub == lane, tail, lower.T)
    out[:half, :] = jnp.where((sub == lane)[:half], lower[:half], out[:half, :])


def unpack_call(packed):
    size = packed.shape[1]
    return pl.pallas_call(
        unpack_kernel,
        out_shape=jax.ShapeDtypeStruct((size, size), jnp.float32),
        in_specs=vmem(1),
        out_specs=vmem(1)[0],
        compiler_params=pltpu.CompilerParams(vmem_limit_bytes=GRANT),
        name="unpack",
    )(packed)


def schur_kernel(groups, width, offsets, pieces, total, arrived, gathered, send1, recv1, send2, recv2):
    grp = lax.axis_index("grp")
    sep = lax.axis_index("sep")
    barrier = pltpu.get_barrier_semaphore()
    for offset in offsets[1:]:
        pl.semaphore_signal(barrier, inc=1, device_id=(grp, (sep + offset) % width), device_id_type=MESH)
    for hop in range(1, groups):
        pl.semaphore_signal(barrier, inc=1, device_id=((grp + hop) % groups, sep), device_id_type=MESH)
    pl.semaphore_wait(barrier, len(offsets) - 1 + groups - 1)
    first = []
    for n, offset in enumerate(offsets[1:]):
        copy = pltpu.make_async_remote_copy(
            src_ref=pieces.at[n + 1],
            dst_ref=arrived.at[n],
            send_sem=send1.at[n],
            recv_sem=recv1.at[n],
            device_id=(grp, (sep + offset) % width),
            device_id_type=MESH,
        )
        copy.start()
        first.append(copy)
    for copy in first:
        copy.wait_recv()
    local = pieces[0]
    for n in range(len(first)):
        local = local + arrived[n]
    gathered[grp] = local
    second = []
    for hop in range(1, groups):
        copy = pltpu.make_async_remote_copy(
            src_ref=gathered.at[grp],
            dst_ref=gathered.at[grp],
            send_sem=send2.at[hop - 1],
            recv_sem=recv2.at[hop - 1],
            device_id=((grp + hop) % groups, sep),
            device_id_type=MESH,
        )
        copy.start()
        second.append(copy)
    for copy in first:
        copy.wait_send()
    for copy in second:
        copy.wait_recv()
    summed = gathered[0]
    for g in range(1, groups):
        summed = summed + gathered[g]
    total[...] = summed
    for copy in second:
        copy.wait_send()


def schur_call(pieces, groups, width, offsets):
    _, height, size = pieces.shape
    partners = len(offsets) - 1
    return pl.pallas_call(
        functools.partial(schur_kernel, groups, width, offsets),
        out_shape=jax.ShapeDtypeStruct((height, size), jnp.float32),
        in_specs=vmem(1),
        out_specs=vmem(1)[0],
        scratch_shapes=[
            pltpu.VMEM((partners, height, size), jnp.float32),
            pltpu.VMEM((groups, height, size), jnp.float32),
            pltpu.SemaphoreType.DMA((partners,)),
            pltpu.SemaphoreType.DMA((partners,)),
            pltpu.SemaphoreType.DMA((groups - 1,)),
            pltpu.SemaphoreType.DMA((groups - 1,)),
        ],
        compiler_params=pltpu.CompilerParams(collective_id=1, has_side_effects=True, vmem_limit_bytes=GRANT),
        name="sums",
    )(pieces)


def body(groups, width, tiles, tile_front, tile_pos, front_slot, front_parent, pivot):
    held = tiles.shape[1]
    room = max(2, -(-2 * held // width))
    offsets = (0, 1, width - 1, width // 2)
    slots = front_slot[0]
    outgoing, labels = pack_call(tile_front.reshape(held), tile_pos[0], slots, tiles[0], width, room)
    arrived, codes = exchange_call(outgoing, labels)
    factor, pieces = front_call(slots, front_parent[0], codes, arrived, pivot[0], offsets, room)
    packed = schur_call(pieces, groups, width, offsets)
    return (factor[None, None], unpack_call(packed)[None])


def solution(mesh):
    placed = (
        P("grp", "sep", None, None),
        P("grp", "sep", None),
        P("grp", "sep"),
        P("grp", None),
        P("grp", None),
        P("grp", None, None),
    )
    return jax.shard_map(
        functools.partial(body, mesh.shape["grp"], mesh.shape["sep"]),
        mesh=mesh,
        in_specs=placed,
        out_specs=(P("grp", "sep", None, None), P("sep", None, None)),
        check_vma=False,
    )
```

```python
import functools
import jax
import jax.numpy as jnp
from jax import lax
from jax.experimental import pallas as pl
from jax.experimental.pallas import tpu as pltpu
from jax.sharding import PartitionSpec as P

MESH = pl.DeviceIdType.MESH

PANEL = 8
GRANT = 20 * 1024 * 1024


def dot_nt(a, b):
    return lax.dot_general(a, b, (((1,), (1,)), ((), ())), precision=lax.Precision.HIGHEST, preferred_element_type=jnp.float32)


def lanes(x, j):
    return jnp.broadcast_to(x[:, j : j + 1], x.shape)


def sublanes(x, r):
    return jnp.broadcast_to(x[r : r + 1, :], x.shape)


def corner(x, s, j):
    return jnp.take_along_axis(lanes(x, j), jnp.full(x.shape, s, jnp.int32), axis=0)


def factor_diagonal(a_ref, u_ref, w_ref):
    size = a_ref.shape[0]
    panels = size // PANEL
    sub = lax.broadcasted_iota(jnp.int32, (PANEL, size), 0)
    lane = lax.broadcasted_iota(jnp.int32, (PANEL, size), 1)
    a = [a_ref[PANEL * i : PANEL * (i + 1), :] for i in range(panels)]
    w = [jnp.where(lane == sub + PANEL * i, 1.0, 0.0) for i in range(panels)]
    for p in range(panels):
        j0 = PANEL * p
        ta = [sublanes(a[p], r) for r in range(PANEL)]
        b = [[corner(a[p], s, j0 + r) for s in range(r + 1)] for r in range(PANEL)]
        tw = [sublanes(w[p], r) for r in range(PANEL)]
        idet = [None] * PANEL
        m = [[None] * PANEL for _ in range(PANEL)]
        for r in range(0, PANEL, 2):
            q = r + 1
            idet[r] = 1.0 / (b[r][r] * b[q][q] - b[q][r] * b[q][r])
            for s in range(r + 2, PANEL):
                m[s][r] = (b[s][r] * b[q][q] - b[s][q] * b[q][r]) * idet[r]
                m[s][q] = (b[s][q] * b[r][r] - b[s][r] * b[q][r]) * idet[r]
            for s in range(r + 2, PANEL):
                for t in range(r + 2, s + 1):
                    b[s][t] = b[s][t] - (m[s][r] * b[t][r] + m[s][q] * b[t][q])
            for s in range(r + 2, PANEL):
                ta[s] = ta[s] - (m[s][r] * ta[r] + m[s][q] * ta[q])
                tw[s] = tw[s] - (m[s][r] * tw[r] + m[s][q] * tw[q])
        u = v = None
        for r in range(0, PANEL, 2):
            q = r + 1
            lead = lax.rsqrt(b[r][r])
            ratio = b[q][r] / b[r][r]
            root = lax.rsqrt(b[q][q] - ratio * b[q][r])
            ua, va = ta[r] * lead, tw[r] * lead
            ub, vb = (ta[q] - ratio * ta[r]) * root, (tw[q] - ratio * tw[r]) * root
            u = ua if r == 0 else jnp.where(sub == r, ua, u)
            v = va if r == 0 else jnp.where(sub == r, va, v)
            u = jnp.where(sub == q, ub, u)
            v = jnp.where(sub == q, vb, v)
        u_ref[j0 : j0 + PANEL, :] = jnp.where(lane >= sub + j0, u, 0.0)
        w_ref[j0 : j0 + PANEL, :] = v
        if p + 1 < panels:
            ya = [None] * PANEL
            yw = [None] * PANEL
            for r in range(0, PANEL, 2):
                q = r + 1
                x, y, z = b[r][r] * idet[r], b[q][r] * idet[r], b[q][q] * idet[r]
                for got, t in ((ya, ta), (yw, tw)):
                    got[r] = z * t[r] - y * t[q]
                    got[q] = x * t[q] - y * t[r]
            for r in reversed(range(0, PANEL, 2)):
                for s in range(r):
                    ya[s] = ya[s] - (m[r][s] * ya[r] + m[r + 1][s] * ya[r + 1])
                    yw[s] = yw[s] - (m[r][s] * yw[r] + m[r + 1][s] * yw[r + 1])
            for i in range(p + 1, panels):
                for s in range(PANEL):
                    c = lanes(a[i], j0 + s)
                    a_new = c * ya[s] if s == 0 else a_new + c * ya[s]
                    w_new = c * yw[s] if s == 0 else w_new + c * yw[s]
                a[i] = a[i] - a_new
                w[i] = w[i] - w_new


def front_kernel(offsets, room, slots, parents, labels, tiles, pivots, factor_ref, pieces_ref, codes, acc, diag, up, winv, schur_ref, sem):
    width, _, rows, size = tiles.shape
    blocks = acc.shape[0]
    elim = blocks - 1
    me = lax.axis_index("sep")
    fetch = pltpu.make_async_copy(labels, codes, sem)
    fetch.start()
    acc[...] = jnp.zeros_like(acc)
    front = 0
    parent = 0
    for f in range(pivots.shape[0]):
        hit = slots[f] == me
        front = jnp.where(hit, f, front)
        parent = jnp.where(hit, parents[f], parent)
    distance = parent - me
    distance = jnp.where(distance < 0, distance + width, distance)
    fetch.wait()

    def add_tiles(s, carry):
        for t in range(room):
            code = codes[s, 0, t]
            r = pl.multiple_of((code >> 3) * rows, rows)
            acc[code & 7, pl.ds(r, rows), :] += tiles[s, t].astype(jnp.float32)
        return carry

    lax.fori_loop(0, width, add_tiles, 0)

    sub = lax.broadcasted_iota(jnp.int32, (size, size), 0)
    lane = lax.broadcasted_iota(jnp.int32, (size, size), 1)

    def span(i):
        return slice(i * size, (i + 1) * size)

    picked = lax.broadcasted_iota(jnp.int32, (pivots.shape[0], size), 0) == front
    row_sums = [jnp.zeros((size, 1), jnp.float32) for _ in range(blocks)]
    for j in range(elim):
        f = acc[j, span(j), :]
        mixed = jnp.where(sub == lane, 0.0, 0.5 * (f + f.T))
        sums = jnp.sum(jnp.where(picked, pivots[:, span(j)], 0.0), 0, keepdims=True) + jnp.sum(mixed, 0, keepdims=True)
        for i in range(j + 1, blocks):
            half = 0.5 * acc[j, span(i), :]
            sums = sums + jnp.sum(half, 0, keepdims=True)
            if i < elim:
                row_sums[i] = row_sums[i] + jnp.sum(half, 1, keepdims=True)
            acc[j, span(i), :] = -half
        acc[j, span(j), :] = jnp.where(sub == lane, sums + row_sums[j], -mixed)

    def step(k, carry):
        diag[...] = acc[k, pl.ds(pl.multiple_of(k * size, size), size), :]
        factor_diagonal(diag, up, winv)
        for kk in range(elim):
            @pl.when(k == kk)
            def _():
                w = winv[...]
                factor_ref[span(kk), span(kk)] = up[...].T
                for j in range(kk + 1, elim):
                    factor_ref[span(kk), span(j)] = jnp.zeros((size, size), jnp.float32)
                below = dot_nt(acc[kk, (kk + 1) * size : blocks * size, :], w)
                factor_ref[(kk + 1) * size : blocks * size, span(kk)] = below
                for j in range(kk + 1, elim):
                    o = (j - kk - 1) * size
                    acc[j, j * size : blocks * size, :] -= dot_nt(below[o:, :], below[o : o + size, :])
                last = below[(elim - kk - 1) * size :, :]
                if kk == 0:
                    schur_ref[...] = dot_nt(last, last)
                else:
                    schur_ref[...] += dot_nt(last, last)
        return carry

    lax.fori_loop(0, elim, step, 0)
    half = size // 2
    sub = lax.broadcasted_iota(jnp.int32, (half, size), 0)
    lane = lax.broadcasted_iota(jnp.int32, (half, size), 1)
    top = pltpu.roll(schur_ref[:half, :], half, 1)
    bottom = schur_ref[half:, :]
    packed = jnp.where((lane < half) | (lane - half > sub), bottom, top)
    tail = jnp.sum(jnp.where(lane - half == sub, bottom, 0.0), 0, keepdims=True)
    tail = jnp.broadcast_to(tail, (8, size))
    for n, offset in enumerate(offsets):
        pieces_ref[n, :half, :] = jnp.where(distance == offset, packed, 0.0)
        pieces_ref[n, half:, :] = jnp.where(distance == offset, tail, 0.0)


def vmem(count):
    return [pl.BlockSpec(memory_space=pltpu.VMEM)] * count


def smem(count):
    return [pl.BlockSpec(memory_space=pltpu.SMEM)] * count


def front_call(slots, parents, labels, tiles, pivots, offsets, room):
    width, _, rows, columns = tiles.shape
    order = pivots.shape[1]
    square = pltpu.VMEM((columns, columns), jnp.float32)
    return pl.pallas_call(
        functools.partial(front_kernel, offsets, room),
        out_shape=(
            jax.ShapeDtypeStruct((order, order - columns), jnp.float32),
            jax.ShapeDtypeStruct((len(offsets), columns // 2 + 8, columns), jnp.float32),
        ),
        in_specs=smem(2) + vmem(3),
        out_specs=vmem(2),
        scratch_shapes=[
            pltpu.SMEM(labels.shape, jnp.int32),
            pltpu.VMEM((order // columns, order + rows, columns), jnp.float32),
            square,
            square,
            square,
            square,
            pltpu.SemaphoreType.DMA,
        ],
        compiler_params=pltpu.CompilerParams(vmem_limit_bytes=GRANT),
        name="front",
    )(slots, parents, labels, tiles, pivots)


def position_codes(positions, rows, columns):
    ratio = columns // rows
    row_count = 5 * ratio
    starts = [0]
    for r in range(row_count):
        starts.append(starts[-1] + r // ratio + 1)
    row = sum((positions >= starts[r]).astype(jnp.int32) for r in range(1, row_count))
    begin = sum(jnp.where(positions >= starts[r], starts[r] - starts[r - 1], 0) for r in range(1, row_count))
    return jnp.where(positions < 0, row_count * 8, row * 8 + positions - begin)


def pack_kernel(fronts_in, positions_in, slots_in, tiles_in, outgoing, labels, fronts, positions, slots, tiles, counts, sem):
    pairs = ((tiles_in, tiles), (fronts_in, fronts), (positions_in, positions), (slots_in, slots))
    copies = [pltpu.make_async_copy(src, dst, sem.at[n]) for n, (src, dst) in enumerate(pairs)]
    for copy in copies:
        copy.start()
    width = outgoing.shape[0]
    held, rows, columns = tiles.shape
    labels[...] = jnp.full(labels.shape, -1, jnp.int32)
    lane = lax.broadcasted_iota(jnp.int32, labels.shape[1:], 1)
    for d in range(width):
        counts[d] = 0
    for copy in copies:
        copy.wait()

    def place(i, carry):
        owner = slots[0, fronts[0, i]]
        rank = counts[owner]
        counts[owner] = rank + 1
        outgoing[owner, rank] = tiles[i]
        labels[owner] = jnp.where(lane == rank, positions[0, i], labels[owner])
        return carry

    lax.fori_loop(0, held, place, 0, unroll=4)
    labels[...] = position_codes(labels[...], rows, columns)


def pack_call(fronts, positions, slots, tiles, width, room):
    held, rows, columns = tiles.shape
    return pl.pallas_call(
        pack_kernel,
        out_shape=(
            jax.ShapeDtypeStruct((width, room, rows, columns), tiles.dtype),
            jax.ShapeDtypeStruct((width, 1, 128), jnp.int32),
        ),
        in_specs=[pl.BlockSpec(memory_space=pltpu.HBM)] * 4,
        out_specs=vmem(2),
        scratch_shapes=[
            pltpu.SMEM(fronts.shape, jnp.int32),
            pltpu.SMEM(positions.shape, jnp.int32),
            pltpu.SMEM(slots.shape, jnp.int32),
            pltpu.VMEM(tiles.shape, tiles.dtype),
            pltpu.SMEM((width,), jnp.int32),
            pltpu.SemaphoreType.DMA((4,)),
        ],
        compiler_params=pltpu.CompilerParams(vmem_limit_bytes=GRANT),
        name="pack",
    )(*(pltpu.with_memory_space_constraint(x, pltpu.HBM) for x in (fronts, positions, slots, tiles)))


def exchange_kernel(width, order, outgoing, labels, arrived, codes, send, recv, lsend, lrecv, own):
    grp = lax.axis_index("grp")
    sep = lax.axis_index("sep")
    barrier = pltpu.get_barrier_semaphore()
    bits = [1 << b for b in range(width.bit_length() - 1)]
    if width == 1 << len(bits):
        partners = [sum(((sep // b) % 2 + (h // b) % 2) % 2 * b for b in bits) for h in order]
    else:
        partners = [(sep + h) % width for h in order]
    for partner in partners:
        pl.semaphore_signal(barrier, inc=1, device_id=(grp, partner), device_id_type=MESH)
    mine = pltpu.make_async_copy(outgoing.at[sep], arrived.at[sep], own.at[0])
    mine.start()
    named = pltpu.make_async_copy(labels.at[sep], codes.at[sep], own.at[1])
    named.start()
    pl.semaphore_wait(barrier, width - 1)
    copies = []
    for n, partner in enumerate(partners):
        for src, dst, s, r in ((outgoing, arrived, send, recv), (labels, codes, lsend, lrecv)):
            copy = pltpu.make_async_remote_copy(
                src_ref=src.at[partner],
                dst_ref=dst.at[sep],
                send_sem=s.at[n],
                recv_sem=r.at[n],
                device_id=(grp, partner),
                device_id_type=MESH,
            )
            copy.start()
            copies.append(copy)
    mine.wait()
    named.wait()
    for copy in copies:
        copy.wait()


def exchange_call(outgoing, labels):
    width = outgoing.shape[0]
    partners = width - 1
    order = sorted(range(1, width), key=lambda h: (-bin(h >> 1).count("1"), h))
    return pl.pallas_call(
        functools.partial(exchange_kernel, width, order),
        out_shape=(
            jax.ShapeDtypeStruct(outgoing.shape, outgoing.dtype),
            jax.ShapeDtypeStruct(labels.shape, labels.dtype),
        ),
        in_specs=vmem(2),
        out_specs=vmem(2),
        scratch_shapes=[pltpu.SemaphoreType.DMA((partners,))] * 4 + [pltpu.SemaphoreType.DMA((2,))],
        compiler_params=pltpu.CompilerParams(collective_id=2, has_side_effects=True, vmem_limit_bytes=GRANT),
        name="exchange",
    )(outgoing, labels)


def unpack_kernel(packed, out):
    size = packed.shape[1]
    half = size // 2
    sub = lax.broadcasted_iota(jnp.int32, (half, size), 0)
    lane = lax.broadcasted_iota(jnp.int32, (half, size), 1)
    body = packed[:half, :]
    top = pltpu.roll(jnp.where((lane >= half) & (lane - half <= sub), body, 0.0), half, 1)
    bottom = jnp.where((lane < half) | (lane - half > sub), body, 0.0)
    lower = jnp.concatenate([top, bottom], 0)
    sub = lax.broadcasted_iota(jnp.int32, (size, size), 0)
    lane = lax.broadcasted_iota(jnp.int32, (size, size), 1)
    tail = jnp.where(lane >= half, packed[half : half + 1, :], 0.0)
    out[...] = lower + jnp.where(sub == lane, tail, lower.T)
    out[:half, :] = jnp.where((sub == lane)[:half], lower[:half], out[:half, :])


def unpack_call(packed):
    size = packed.shape[1]
    return pl.pallas_call(
        unpack_kernel,
        out_shape=jax.ShapeDtypeStruct((size, size), jnp.float32),
        in_specs=vmem(1),
        out_specs=vmem(1)[0],
        compiler_params=pltpu.CompilerParams(vmem_limit_bytes=GRANT),
        name="unpack",
    )(packed)


def schur_kernel(groups, width, offsets, pieces, total, arrived, gathered, send1, recv1, send2, recv2):
    grp = lax.axis_index("grp")
    sep = lax.axis_index("sep")
    barrier = pltpu.get_barrier_semaphore()
    for offset in offsets[1:]:
        pl.semaphore_signal(barrier, inc=1, device_id=(grp, (sep + offset) % width), device_id_type=MESH)
    for hop in range(1, groups):
        pl.semaphore_signal(barrier, inc=1, device_id=((grp + hop) % groups, sep), device_id_type=MESH)
    pl.semaphore_wait(barrier, len(offsets) - 1 + groups - 1)
    first = []
    for n, offset in enumerate(offsets[1:]):
        copy = pltpu.make_async_remote_copy(
            src_ref=pieces.at[n + 1],
            dst_ref=arrived.at[n],
            send_sem=send1.at[n],
            recv_sem=recv1.at[n],
            device_id=(grp, (sep + offset) % width),
            device_id_type=MESH,
        )
        copy.start()
        first.append(copy)
    for copy in first:
        copy.wait_recv()
    local = pieces[0]
    for n in range(len(first)):
        local = local + arrived[n]
    gathered[grp] = local
    second = []
    for hop in range(1, groups):
        copy = pltpu.make_async_remote_copy(
            src_ref=gathered.at[grp],
            dst_ref=gathered.at[grp],
            send_sem=send2.at[hop - 1],
            recv_sem=recv2.at[hop - 1],
            device_id=((grp + hop) % groups, sep),
            device_id_type=MESH,
        )
        copy.start()
        second.append(copy)
    for copy in first:
        copy.wait_send()
    for copy in second:
        copy.wait_recv()
    summed = gathered[0]
    for g in range(1, groups):
        summed = summed + gathered[g]
    total[...] = summed
    for copy in second:
        copy.wait_send()


def schur_call(pieces, groups, width, offsets):
    _, height, size = pieces.shape
    partners = len(offsets) - 1
    return pl.pallas_call(
        functools.partial(schur_kernel, groups, width, offsets),
        out_shape=jax.ShapeDtypeStruct((height, size), jnp.float32),
        in_specs=vmem(1),
        out_specs=vmem(1)[0],
        scratch_shapes=[
            pltpu.VMEM((partners, height, size), jnp.float32),
            pltpu.VMEM((groups, height, size), jnp.float32),
            pltpu.SemaphoreType.DMA((partners,)),
            pltpu.SemaphoreType.DMA((partners,)),
            pltpu.SemaphoreType.DMA((groups - 1,)),
            pltpu.SemaphoreType.DMA((groups - 1,)),
        ],
        compiler_params=pltpu.CompilerParams(collective_id=1, has_side_effects=True, vmem_limit_bytes=GRANT),
        name="sums",
    )(pieces)


def body(groups, width, tiles, tile_front, tile_pos, front_slot, front_parent, pivot):
    held = tiles.shape[1]
    room = max(2, -(-2 * held // width))
    offsets = (0, 1, width - 1, width // 2)
    slots = front_slot[0]
    outgoing, labels = pack_call(tile_front.reshape(1, held), tile_pos, front_slot, tiles[0], width, room)
    arrived, codes = exchange_call(outgoing, labels)
    factor, pieces = front_call(slots, front_parent[0], codes, arrived, pivot[0], offsets, room)
    packed = schur_call(pieces, groups, width, offsets)
    return (factor[None, None], unpack_call(packed)[None])


def solution(mesh):
    placed = (
        P("grp", "sep", None, None),
        P("grp", "sep", None),
        P("grp", "sep"),
        P("grp", None),
        P("grp", None),
        P("grp", None, None),
    )
    return jax.shard_map(
        functools.partial(body, mesh.shape["grp"], mesh.shape["sep"]),
        mesh=mesh,
        in_specs=placed,
        out_specs=(P("grp", "sep", None, None), P("sep", None, None)),
        check_vma=False,
    )
```

```python
import functools
import jax
import jax.numpy as jnp
from jax import lax
from jax.experimental import pallas as pl
from jax.experimental.pallas import tpu as pltpu
from jax.sharding import PartitionSpec as P

MESH = pl.DeviceIdType.MESH

PANEL = 8
GRANT = 20 * 1024 * 1024


def dot_nt(a, b):
    return lax.dot_general(a, b, (((1,), (1,)), ((), ())), precision=lax.Precision.HIGHEST, preferred_element_type=jnp.float32)


def lanes(x, j):
    return jnp.broadcast_to(x[:, j : j + 1], x.shape)


def sublanes(x, r):
    return jnp.broadcast_to(x[r : r + 1, :], x.shape)


def corner(x, s, j):
    return jnp.take_along_axis(lanes(x, j), jnp.full(x.shape, s, jnp.int32), axis=0)


def factor_diagonal(a_ref, u_ref, w_ref):
    size = a_ref.shape[0]
    panels = size // PANEL
    sub = lax.broadcasted_iota(jnp.int32, (PANEL, size), 0)
    lane = lax.broadcasted_iota(jnp.int32, (PANEL, size), 1)
    a = [a_ref[PANEL * i : PANEL * (i + 1), :] for i in range(panels)]
    w = [jnp.where(lane == sub + PANEL * i, 1.0, 0.0) for i in range(panels)]
    for p in range(panels):
        j0 = PANEL * p
        ta = [sublanes(a[p], r) for r in range(PANEL)]
        b = [[corner(a[p], s, j0 + r) for s in range(r + 1)] for r in range(PANEL)]
        tw = [sublanes(w[p], r) for r in range(PANEL)]
        idet = [None] * PANEL
        m = [[None] * PANEL for _ in range(PANEL)]
        for r in range(0, PANEL, 2):
            q = r + 1
            idet[r] = 1.0 / (b[r][r] * b[q][q] - b[q][r] * b[q][r])
            for s in range(r + 2, PANEL):
                m[s][r] = (b[s][r] * b[q][q] - b[s][q] * b[q][r]) * idet[r]
                m[s][q] = (b[s][q] * b[r][r] - b[s][r] * b[q][r]) * idet[r]
            for s in range(r + 2, PANEL):
                for t in range(r + 2, s + 1):
                    b[s][t] = b[s][t] - (m[s][r] * b[t][r] + m[s][q] * b[t][q])
            for s in range(r + 2, PANEL):
                ta[s] = ta[s] - (m[s][r] * ta[r] + m[s][q] * ta[q])
                tw[s] = tw[s] - (m[s][r] * tw[r] + m[s][q] * tw[q])
        u = v = None
        for r in range(0, PANEL, 2):
            q = r + 1
            lead = lax.rsqrt(b[r][r])
            ratio = b[q][r] / b[r][r]
            root = lax.rsqrt(b[q][q] - ratio * b[q][r])
            ua, va = ta[r] * lead, tw[r] * lead
            ub, vb = (ta[q] - ratio * ta[r]) * root, (tw[q] - ratio * tw[r]) * root
            u = ua if r == 0 else jnp.where(sub == r, ua, u)
            v = va if r == 0 else jnp.where(sub == r, va, v)
            u = jnp.where(sub == q, ub, u)
            v = jnp.where(sub == q, vb, v)
        u_ref[j0 : j0 + PANEL, :] = jnp.where(lane >= sub + j0, u, 0.0)
        w_ref[j0 : j0 + PANEL, :] = v
        if p + 1 < panels:
            ya = [None] * PANEL
            yw = [None] * PANEL
            for r in range(0, PANEL, 2):
                q = r + 1
                x, y, z = b[r][r] * idet[r], b[q][r] * idet[r], b[q][q] * idet[r]
                for got, t in ((ya, ta), (yw, tw)):
                    got[r] = z * t[r] - y * t[q]
                    got[q] = x * t[q] - y * t[r]
            for r in reversed(range(0, PANEL, 2)):
                for s in range(r):
                    ya[s] = ya[s] - (m[r][s] * ya[r] + m[r + 1][s] * ya[r + 1])
                    yw[s] = yw[s] - (m[r][s] * yw[r] + m[r + 1][s] * yw[r + 1])
            for i in range(p + 1, panels):
                for s in range(PANEL):
                    c = lanes(a[i], j0 + s)
                    a_new = c * ya[s] if s == 0 else a_new + c * ya[s]
                    w_new = c * yw[s] if s == 0 else w_new + c * yw[s]
                a[i] = a[i] - a_new
                w[i] = w[i] - w_new


def front_kernel(offsets, room, slots, parents, labels, tiles, pivots, factor_out, pieces_ref, codes, acc, diag, up, winv, schur_ref, sem, factor_ref, written):
    width, _, rows, size = tiles.shape
    blocks = acc.shape[0]
    elim = blocks - 1
    me = lax.axis_index("sep")
    fetch = pltpu.make_async_copy(labels, codes, sem)
    fetch.start()
    acc[...] = jnp.zeros_like(acc)
    front = 0
    parent = 0
    for f in range(pivots.shape[0]):
        hit = slots[f] == me
        front = jnp.where(hit, f, front)
        parent = jnp.where(hit, parents[f], parent)
    distance = parent - me
    distance = jnp.where(distance < 0, distance + width, distance)
    fetch.wait()

    def add_tiles(s, carry):
        for t in range(room):
            code = codes[s, 0, t]
            r = pl.multiple_of((code >> 3) * rows, rows)
            acc[code & 7, pl.ds(r, rows), :] += tiles[s, t].astype(jnp.float32)
        return carry

    lax.fori_loop(0, width, add_tiles, 0)

    sub = lax.broadcasted_iota(jnp.int32, (size, size), 0)
    lane = lax.broadcasted_iota(jnp.int32, (size, size), 1)

    def span(i):
        return slice(i * size, (i + 1) * size)

    picked = lax.broadcasted_iota(jnp.int32, (pivots.shape[0], size), 0) == front
    row_sums = [jnp.zeros((size, 1), jnp.float32) for _ in range(blocks)]
    for j in range(elim):
        f = acc[j, span(j), :]
        mixed = jnp.where(sub == lane, 0.0, 0.5 * (f + f.T))
        sums = jnp.sum(jnp.where(picked, pivots[:, span(j)], 0.0), 0, keepdims=True) + jnp.sum(mixed, 0, keepdims=True)
        for i in range(j + 1, blocks):
            half = 0.5 * acc[j, span(i), :]
            sums = sums + jnp.sum(half, 0, keepdims=True)
            if i < elim:
                row_sums[i] = row_sums[i] + jnp.sum(half, 1, keepdims=True)
            acc[j, span(i), :] = -half
        acc[j, span(j), :] = jnp.where(sub == lane, sums + row_sums[j], -mixed)

    def write(j):
        return pltpu.make_async_copy(factor_ref.at[:, span(j)], factor_out.at[:, span(j)], written.at[j])

    def step(k, carry):
        diag[...] = acc[k, pl.ds(pl.multiple_of(k * size, size), size), :]
        factor_diagonal(diag, up, winv)
        for kk in range(elim):
            @pl.when(k == kk)
            def _():
                w = winv[...]
                factor_ref[span(kk), span(kk)] = up[...].T
                for j in range(kk + 1, elim):
                    factor_ref[span(kk), span(j)] = jnp.zeros((size, size), jnp.float32)
                below = dot_nt(acc[kk, (kk + 1) * size : blocks * size, :], w)
                factor_ref[(kk + 1) * size : blocks * size, span(kk)] = below
                for j in range(kk + 1, elim):
                    o = (j - kk - 1) * size
                    acc[j, j * size : blocks * size, :] -= dot_nt(below[o:, :], below[o : o + size, :])
                write(kk).start()
                last = below[(elim - kk - 1) * size :, :]
                if kk == 0:
                    schur_ref[...] = dot_nt(last, last)
                else:
                    schur_ref[...] += dot_nt(last, last)
        return carry

    lax.fori_loop(0, elim, step, 0)
    half = size // 2
    sub = lax.broadcasted_iota(jnp.int32, (half, size), 0)
    lane = lax.broadcasted_iota(jnp.int32, (half, size), 1)
    top = pltpu.roll(schur_ref[:half, :], half, 1)
    bottom = schur_ref[half:, :]
    packed = jnp.where((lane < half) | (lane - half > sub), bottom, top)
    tail = jnp.sum(jnp.where(lane - half == sub, bottom, 0.0), 0, keepdims=True)
    tail = jnp.broadcast_to(tail, (8, size))
    for n, offset in enumerate(offsets):
        pieces_ref[n, :half, :] = jnp.where(distance == offset, packed, 0.0)
        pieces_ref[n, half:, :] = jnp.where(distance == offset, tail, 0.0)
    for j in range(elim):
        write(j).wait()


def vmem(count):
    return [pl.BlockSpec(memory_space=pltpu.VMEM)] * count


def smem(count):
    return [pl.BlockSpec(memory_space=pltpu.SMEM)] * count


def front_call(slots, parents, labels, tiles, pivots, offsets, room):
    width, _, rows, columns = tiles.shape
    order = pivots.shape[1]
    square = pltpu.VMEM((columns, columns), jnp.float32)
    return pl.pallas_call(
        functools.partial(front_kernel, offsets, room),
        out_shape=(
            jax.ShapeDtypeStruct((order, order - columns), jnp.float32),
            jax.ShapeDtypeStruct((len(offsets), columns // 2 + 8, columns), jnp.float32),
        ),
        in_specs=smem(2) + vmem(3),
        out_specs=[pl.BlockSpec(memory_space=pltpu.HBM)] + vmem(1),
        scratch_shapes=[
            pltpu.SMEM(labels.shape, jnp.int32),
            pltpu.VMEM((order // columns, order + rows, columns), jnp.float32),
            square,
            square,
            square,
            square,
            pltpu.SemaphoreType.DMA,
            pltpu.VMEM((order, order - columns), jnp.float32),
            pltpu.SemaphoreType.DMA((order // columns - 1,)),
        ],
        compiler_params=pltpu.CompilerParams(vmem_limit_bytes=GRANT),
        name="front",
    )(slots, parents, labels, tiles, pivots)


def position_codes(positions, rows, columns):
    ratio = columns // rows
    row_count = 5 * ratio
    starts = [0]
    for r in range(row_count):
        starts.append(starts[-1] + r // ratio + 1)
    row = sum((positions >= starts[r]).astype(jnp.int32) for r in range(1, row_count))
    begin = sum(jnp.where(positions >= starts[r], starts[r] - starts[r - 1], 0) for r in range(1, row_count))
    return jnp.where(positions < 0, row_count * 8, row * 8 + positions - begin)


def pack_kernel(fronts_in, positions_in, slots_in, tiles_in, outgoing, labels, fronts, positions, slots, tiles, counts, sem):
    pairs = ((tiles_in, tiles), (fronts_in, fronts), (positions_in, positions), (slots_in, slots))
    copies = [pltpu.make_async_copy(src, dst, sem.at[n]) for n, (src, dst) in enumerate(pairs)]
    for copy in copies:
        copy.start()
    width = outgoing.shape[0]
    held, rows, columns = tiles.shape
    labels[...] = jnp.full(labels.shape, -1, jnp.int32)
    lane = lax.broadcasted_iota(jnp.int32, labels.shape[1:], 1)
    for d in range(width):
        counts[d] = 0
    for copy in copies:
        copy.wait()

    def place(i, carry):
        owner = slots[0, fronts[0, i]]
        rank = counts[owner]
        counts[owner] = rank + 1
        outgoing[owner, rank] = tiles[i]
        labels[owner] = jnp.where(lane == rank, positions[0, i], labels[owner])
        return carry

    lax.fori_loop(0, held, place, 0, unroll=4)
    labels[...] = position_codes(labels[...], rows, columns)


def pack_call(fronts, positions, slots, tiles, width, room):
    held, rows, columns = tiles.shape
    return pl.pallas_call(
        pack_kernel,
        out_shape=(
            jax.ShapeDtypeStruct((width, room, rows, columns), tiles.dtype),
            jax.ShapeDtypeStruct((width, 1, 128), jnp.int32),
        ),
        in_specs=[pl.BlockSpec(memory_space=pltpu.HBM)] * 4,
        out_specs=vmem(2),
        scratch_shapes=[
            pltpu.SMEM(fronts.shape, jnp.int32),
            pltpu.SMEM(positions.shape, jnp.int32),
            pltpu.SMEM(slots.shape, jnp.int32),
            pltpu.VMEM(tiles.shape, tiles.dtype),
            pltpu.SMEM((width,), jnp.int32),
            pltpu.SemaphoreType.DMA((4,)),
        ],
        compiler_params=pltpu.CompilerParams(vmem_limit_bytes=GRANT),
        name="pack",
    )(*(pltpu.with_memory_space_constraint(x, pltpu.HBM) for x in (fronts, positions, slots, tiles)))


def exchange_kernel(width, order, outgoing, labels, arrived, codes, send, recv, lsend, lrecv, own):
    grp = lax.axis_index("grp")
    sep = lax.axis_index("sep")
    barrier = pltpu.get_barrier_semaphore()
    bits = [1 << b for b in range(width.bit_length() - 1)]
    if width == 1 << len(bits):
        partners = [sum(((sep // b) % 2 + (h // b) % 2) % 2 * b for b in bits) for h in order]
    else:
        partners = [(sep + h) % width for h in order]
    for partner in partners:
        pl.semaphore_signal(barrier, inc=1, device_id=(grp, partner), device_id_type=MESH)
    mine = pltpu.make_async_copy(outgoing.at[sep], arrived.at[sep], own.at[0])
    mine.start()
    named = pltpu.make_async_copy(labels.at[sep], codes.at[sep], own.at[1])
    named.start()
    pl.semaphore_wait(barrier, width - 1)
    copies = []
    for n, partner in enumerate(partners):
        for src, dst, s, r in ((outgoing, arrived, send, recv), (labels, codes, lsend, lrecv)):
            copy = pltpu.make_async_remote_copy(
                src_ref=src.at[partner],
                dst_ref=dst.at[sep],
                send_sem=s.at[n],
                recv_sem=r.at[n],
                device_id=(grp, partner),
                device_id_type=MESH,
            )
            copy.start()
            copies.append(copy)
    mine.wait()
    named.wait()
    for copy in copies:
        copy.wait()


def exchange_call(outgoing, labels):
    width = outgoing.shape[0]
    partners = width - 1
    order = sorted(range(1, width), key=lambda h: (-bin(h >> 1).count("1"), h))
    return pl.pallas_call(
        functools.partial(exchange_kernel, width, order),
        out_shape=(
            jax.ShapeDtypeStruct(outgoing.shape, outgoing.dtype),
            jax.ShapeDtypeStruct(labels.shape, labels.dtype),
        ),
        in_specs=vmem(2),
        out_specs=vmem(2),
        scratch_shapes=[pltpu.SemaphoreType.DMA((partners,))] * 4 + [pltpu.SemaphoreType.DMA((2,))],
        compiler_params=pltpu.CompilerParams(collective_id=2, has_side_effects=True, vmem_limit_bytes=GRANT),
        name="exchange",
    )(outgoing, labels)


def unpack_kernel(packed, out):
    size = packed.shape[1]
    half = size // 2
    sub = lax.broadcasted_iota(jnp.int32, (half, size), 0)
    lane = lax.broadcasted_iota(jnp.int32, (half, size), 1)
    body = packed[:half, :]
    top = pltpu.roll(jnp.where((lane >= half) & (lane - half <= sub), body, 0.0), half, 1)
    bottom = jnp.where((lane < half) | (lane - half > sub), body, 0.0)
    lower = jnp.concatenate([top, bottom], 0)
    sub = lax.broadcasted_iota(jnp.int32, (size, size), 0)
    lane = lax.broadcasted_iota(jnp.int32, (size, size), 1)
    tail = jnp.where(lane >= half, packed[half : half + 1, :], 0.0)
    out[...] = lower + jnp.where(sub == lane, tail, lower.T)
    out[:half, :] = jnp.where((sub == lane)[:half], lower[:half], out[:half, :])


def unpack_call(packed):
    size = packed.shape[1]
    return pl.pallas_call(
        unpack_kernel,
        out_shape=jax.ShapeDtypeStruct((size, size), jnp.float32),
        in_specs=vmem(1),
        out_specs=vmem(1)[0],
        compiler_params=pltpu.CompilerParams(vmem_limit_bytes=GRANT),
        name="unpack",
    )(packed)


def schur_kernel(groups, width, offsets, pieces, total, arrived, gathered, send1, recv1, send2, recv2):
    grp = lax.axis_index("grp")
    sep = lax.axis_index("sep")
    barrier = pltpu.get_barrier_semaphore()
    for offset in offsets[1:]:
        pl.semaphore_signal(barrier, inc=1, device_id=(grp, (sep + offset) % width), device_id_type=MESH)
    for hop in range(1, groups):
        pl.semaphore_signal(barrier, inc=1, device_id=((grp + hop) % groups, sep), device_id_type=MESH)
    pl.semaphore_wait(barrier, len(offsets) - 1 + groups - 1)
    first = []
    for n, offset in enumerate(offsets[1:]):
        copy = pltpu.make_async_remote_copy(
            src_ref=pieces.at[n + 1],
            dst_ref=arrived.at[n],
            send_sem=send1.at[n],
            recv_sem=recv1.at[n],
            device_id=(grp, (sep + offset) % width),
            device_id_type=MESH,
        )
        copy.start()
        first.append(copy)
    for copy in first:
        copy.wait_recv()
    local = pieces[0]
    for n in range(len(first)):
        local = local + arrived[n]
    gathered[grp] = local
    second = []
    for hop in range(1, groups):
        copy = pltpu.make_async_remote_copy(
            src_ref=gathered.at[grp],
            dst_ref=gathered.at[grp],
            send_sem=send2.at[hop - 1],
            recv_sem=recv2.at[hop - 1],
            device_id=((grp + hop) % groups, sep),
            device_id_type=MESH,
        )
        copy.start()
        second.append(copy)
    for copy in first:
        copy.wait_send()
    for copy in second:
        copy.wait_recv()
    summed = gathered[0]
    for g in range(1, groups):
        summed = summed + gathered[g]
    total[...] = summed
    for copy in second:
        copy.wait_send()


def schur_call(pieces, groups, width, offsets):
    _, height, size = pieces.shape
    partners = len(offsets) - 1
    return pl.pallas_call(
        functools.partial(schur_kernel, groups, width, offsets),
        out_shape=jax.ShapeDtypeStruct((height, size), jnp.float32),
        in_specs=vmem(1),
        out_specs=vmem(1)[0],
        scratch_shapes=[
            pltpu.VMEM((partners, height, size), jnp.float32),
            pltpu.VMEM((groups, height, size), jnp.float32),
            pltpu.SemaphoreType.DMA((partners,)),
            pltpu.SemaphoreType.DMA((partners,)),
            pltpu.SemaphoreType.DMA((groups - 1,)),
            pltpu.SemaphoreType.DMA((groups - 1,)),
        ],
        compiler_params=pltpu.CompilerParams(collective_id=1, has_side_effects=True, vmem_limit_bytes=GRANT),
        name="sums",
    )(pieces)


def body(groups, width, tiles, tile_front, tile_pos, front_slot, front_parent, pivot):
    held = tiles.shape[1]
    room = max(2, -(-2 * held // width))
    offsets = (0, 1, width - 1, width // 2)
    slots = front_slot[0]
    outgoing, labels = pack_call(tile_front.reshape(1, held), tile_pos, front_slot, tiles[0], width, room)
    arrived, codes = exchange_call(outgoing, labels)
    factor, pieces = front_call(slots, front_parent[0], codes, arrived, pivot[0], offsets, room)
    packed = schur_call(pieces, groups, width, offsets)
    return (factor[None, None], unpack_call(packed)[None])


def solution(mesh):
    placed = (
        P("grp", "sep", None, None),
        P("grp", "sep", None),
        P("grp", "sep"),
        P("grp", None),
        P("grp", None),
        P("grp", None, None),
    )
    return jax.shard_map(
        functools.partial(body, mesh.shape["grp"], mesh.shape["sep"]),
        mesh=mesh,
        in_specs=placed,
        out_specs=(P("grp", "sep", None, None), P("sep", None, None)),
        check_vma=False,
    )
```
